512 devices in a mesh: grp: 8 (over x, z_lo), req: 64 (over y, z_hi, core).
Axes of the slice: x: 4, y: 8, z: 8 (z_hi: 4, z_lo: 2; z = z_hi * 2 + z_lo), core: 2. Of those that a mesh axis runs over, the one named last changes fastest.
Arguments:
- queries: bfloat16 [8, 8192, 1024], P('grp', 'req')
- suffix_kv: bfloat16 [8, 2, 8192, 1024], P('grp', None, 'req')
- prefix_kv: bfloat16 [8, 2, 1024, 1024], P('grp', None, 'req'), may hold values from -6 to 6
- lengths: int32 [8, 12], P('grp'), may hold values from 1 to 2048, 8192 in all within a row
Outputs:
- attended: bfloat16 [8, 8192, 1024], P('grp', 'req')
The draws below stay inside these ranges and needn't reach their ends.
Inputs may be any that keep to these rules, and one draw needn't show every extreme that they name: Each group's 12 lengths sum to 8192, the longest exactly 2048.
All inputs are finite; a program needn't handle non-finite values.
Results may differ from the reference program's by a relative error of at most 0.0075.
Values may be sent and summed in bfloat16 or wider, within the bound.
A program may use at most 64 MiB of HBM per device.

```python
import math
import jax
import jax.numpy as jnp
import numpy as np
from jax import lax

HEADS = 16
HEAD = 64
WIN = 1024
REQS = 12
GROUPS = 8
SUFFIX = 8192
HD = 1024
MOST = 2048


def shared_keys(key):
    inner = jax.random.fold_in(key, 7)
    values = jax.random.normal(inner, (GROUPS, 2, SUFFIX, HD), jnp.float32)
    values = jnp.clip(values, -6.0, 6.0)
    return values


def draw_suffix_kv(key, part):
    return shared_keys(key).astype(jnp.bfloat16)


def draw_queries(key, part):
    inner = jax.random.fold_in(key, 11)
    base = jnp.clip(jax.random.normal(inner, (GROUPS, SUFFIX, HD), jnp.float32), -6.0, 6.0)
    return base.astype(jnp.bfloat16)


def level_of(stream_key, dims, split, low, largest):
    gain, own = 1.0, jax.random.fold_in(stream_key, 6)
    for axis_at, parts in split:
        draws = jnp.exp(jax.random.uniform(jax.random.fold_in(own, axis_at), (parts,), jnp.float32, low / len(split), largest / len(split)))
        gain = gain * jnp.repeat(draws, dims[axis_at] // parts).reshape([-1 if axis == axis_at else 1 for axis in range(len(dims))])
    return gain


def split_up(amount, total, reach, lean):
    weights = [(1 << 20) // math.isqrt(rank ** lean) + 1 for rank in range(2, amount + 1)]
    spare, given = total - reach - (amount - 1), [1] * (amount - 1)
    while spare > 0:
        movable = [i for i in range(amount - 1) if given[i] < reach]
        mass, remaining = sum([weights[i] for i in movable]), spare
        for i in movable:
            addition = min(reach - given[i], max(1, remaining * weights[i] // mass), spare)
            given[i] = given[i] + addition
            spare = spare - addition
    return np.array([reach] + given)


def ragged(own_key, number_of, total, most, slope):
    if number_of == 2:
        one = jax.random.randint(own_key, (), max(1, total - most), min(most, total - 1) + 1)
        return jnp.stack([one, total - one])
    sizes = jnp.asarray(split_up(number_of, total, most, slope), jnp.int32)
    couples = (number_of - 1) // 2
    donor, taker = sizes[1:1 + 2 * couples:2], sizes[2:2 + 2 * couples:2]
    room = jnp.minimum(donor - 1, most - taker)
    moved = jax.random.randint(jax.random.fold_in(own_key, 1), (couples,), 0, 1 << 20) % (room + 1)
    sizes = sizes.at[1:1 + 2 * couples:2].set(donor - moved).at[2:2 + 2 * couples:2].set(taker + moved)
    return sizes[jax.random.permutation(jax.random.fold_in(own_key, 2), number_of)]


def normal_values(own_key, shape, deviation, limit, split=(), kind=jnp.bfloat16):
    values = deviation * jax.random.normal(own_key, shape, jnp.float32)
    if split:
        values = values * level_of(own_key, shape, split, -0.22, 0.18)
    return jnp.clip(values, -limit, limit).astype(kind)


def setup_inputs(seed: int = 0) -> dict:
    streams_of = jax.random.split(jax.random.key(seed), 5)
    return {
        "queries": draw_queries(jax.random.fold_in(streams_of[4], 71), 0),
        "suffix_kv": draw_suffix_kv(jax.random.fold_in(streams_of[4], 71), 0),
        "prefix_kv": normal_values(streams_of[2], (GROUPS, 2, WIN, HD), 1.0, 6.0, ((0, 8), (2, 64))),
        "lengths": jax.vmap(lambda own: ragged(own, REQS, SUFFIX, MOST, 2))(jax.random.split(streams_of[3], GROUPS)).reshape((GROUPS, REQS)).astype(jnp.int32),
    }


def locate(positions, starts, ends):
    inside = (positions[:, None] >= starts[None, :]) & (positions[:, None] < ends[None, :])
    numbers = jnp.arange(1, starts.shape[0] + 1, dtype=jnp.int32)
    request = jnp.sum(jnp.where(inside, numbers[None, :], 0), axis=1).astype(jnp.int32) - 1
    offset = positions - jnp.sum(jnp.where(inside, starts[None, :], 0), axis=1).astype(jnp.int32)
    return request, offset


def reference(queries, suffix_kv, prefix_kv, lengths):
    block_rows = min(512, SUFFIX)
    results = []
    for group in range(GROUPS):
        lens = lengths[group].astype(jnp.int32)
        ends = jnp.cumsum(lens).astype(jnp.int32)
        starts = ends - lens
        padding = jnp.zeros((2, WIN, HD), jnp.bfloat16)
        padded = jnp.concatenate([padding, suffix_kv[group]], axis=1)
        prefix_keys = prefix_kv[group, 0].astype(jnp.float32).reshape(WIN, HEADS, HEAD)
        prefix_vals = prefix_kv[group, 1].astype(jnp.float32).reshape(WIN, HEADS, HEAD)
        group_queries = queries[group]

        def one_block(number):
            first = (number * block_rows).astype(jnp.int32)
            query = lax.dynamic_slice_in_dim(group_queries, first, block_rows, 0)
            query = query.astype(jnp.float32).reshape(block_rows, HEADS, HEAD)
            near = lax.dynamic_slice_in_dim(padded, first, WIN + block_rows, 1)
            key_index = first - WIN + jnp.arange(WIN + block_rows, dtype=jnp.int32)
            query_index = first + jnp.arange(block_rows, dtype=jnp.int32)
            key_req, key_off = locate(key_index, starts, ends)
            query_req, query_off = locate(query_index, starts, ends)
            near_mask = (key_req[None, :] == query_req[:, None]) & (key_off[None, :] <= query_off[:, None])
            near_mask = near_mask & (query_off[:, None] - key_off[None, :] < WIN) & (key_index[None, :] >= 0)
            prefix_mask = jnp.arange(WIN, dtype=jnp.int32)[None, :] > query_off[:, None]
            mask = jnp.concatenate([prefix_mask, near_mask], axis=1)
            keys = jnp.concatenate([prefix_keys, near[0].astype(jnp.float32).reshape(-1, HEADS, HEAD)], axis=0)
            vals = jnp.concatenate([prefix_vals, near[1].astype(jnp.float32).reshape(-1, HEADS, HEAD)], axis=0)
            score = jnp.einsum("qhd,khd->hqk", query, keys) * 0.125
            score = jnp.where(mask[None], score, -1e30)
            top = jnp.max(score, axis=-1, keepdims=True)
            weight = jnp.where(mask[None], jnp.exp(score - top), 0.0)
            total = jnp.sum(weight, axis=-1)
            rounded = weight.astype(jnp.bfloat16).astype(jnp.float32)
            summed = jnp.einsum("hqk,khd->hqd", rounded, vals) / total[..., None]
            return jnp.transpose(summed, (1, 0, 2)).reshape(block_rows, HD).astype(jnp.bfloat16)

        attended = lax.map(one_block, jnp.arange(SUFFIX // block_rows, dtype=jnp.int32)).reshape(SUFFIX, HD)
        results.append(attended)
    return jnp.stack(results, axis=0)
```

```python
import functools

import jax
import jax.numpy as jnp
from jax import lax
from jax.experimental import pallas as pl
from jax.experimental.pallas import tpu as pltpu
from jax.sharding import PartitionSpec as P

HEADS = 16
HEAD = 64
WIN = 1024
REQS = 12
ROW = 8
RING = 8
TOK = 128
PRE = 16
LANES = 128
MESH = pl.DeviceIdType.MESH


def place():
    grp = lax.axis_index("grp")
    me = lax.axis_index("req")
    return grp, me // ROW, me % ROW


def cols(number):
    return pl.ds(pl.multiple_of(number * LANES, LANES), LANES)


def rows(number, size, base=0):
    return pl.ds(pl.multiple_of(base + number * size, size), size)


def gather_kernel(q_ref, kv_ref, pre_ref, q_out, kv_out, pre_out,
                  q_own, kv_own, pre_own, a2a_send, a2a_recv, fwd_send, fwd_recv,
                  ring_send, ring_recv, local):
    grp, y, s = place()

    def peer(k):
        return (grp, y * ROW + (s + k) % ROW)

    up = (grp, ((y + 1) % RING) * ROW + s)
    down = (grp, ((y + RING - 1) % RING) * ROW + s)

    own_in = [
        pltpu.make_async_copy(pre_ref.at[0, :, :, cols(s)], pre_own, local.at[0]),
        pltpu.make_async_copy(kv_ref.at[0, :, :, cols(s)], kv_own, local.at[1]),
        pltpu.make_async_copy(q_ref.at[0, :, cols(s)], q_own, local.at[2]),
    ]
    for copy in own_in:
        copy.start()

    barrier = pltpu.get_barrier_semaphore()
    for k in range(1, ROW):
        pl.semaphore_signal(barrier, 1, device_id=peer(k), device_id_type=MESH)
    pl.semaphore_signal(barrier, 1, device_id=up, device_id_type=MESH)
    pl.semaphore_signal(barrier, 1, device_id=down, device_id_type=MESH)
    pl.semaphore_wait(barrier, ROW + 1)

    def send(src, dst, send_sem, recv_sem, to):
        copy = pltpu.make_async_remote_copy(
            src, dst, send_sem, recv_sem, device_id=to, device_id_type=MESH)
        copy.start()
        return copy

    order = (4, 2, 6, 3, 5, 1, 7)
    pre_sent = {}
    for k in order:
        t = (s + k) % ROW
        pre_sent[k] = send(pre_ref.at[0, :, :, cols(t)], pre_out.at[:, rows(y * ROW + s, PRE)],
                           a2a_send.at[0, k], a2a_recv.at[0, k], peer(k))
    kv_fwd = {0: send(kv_ref.at[0, :, :, cols(s)], kv_out.at[:, rows(s, TOK)],
                      fwd_send.at[0], fwd_recv.at[0], up)}
    kv_sent = {}
    for k in order:
        t = (s + k) % ROW
        kv_sent[k] = send(kv_ref.at[0, :, :, cols(t)], kv_out.at[:, rows(ROW + s, TOK)],
                          a2a_send.at[1, k], a2a_recv.at[1, k], peer(k))
    q_sent = {}
    for k in order:
        t = (s + k) % ROW
        q_sent[k] = send(q_ref.at[0, :, cols(t)], q_out.at[rows(s, TOK)],
                         a2a_send.at[2, k], a2a_recv.at[2, k], peer(k))
    own_out = [
        pltpu.make_async_copy(pre_own, pre_out.at[:, rows(y * ROW + s, PRE)], local.at[3]),
        pltpu.make_async_copy(kv_own, kv_out.at[:, rows(ROW + s, TOK)], local.at[4]),
        pltpu.make_async_copy(q_own, q_out.at[rows(s, TOK)], local.at[5]),
    ]
    for before, after in zip(own_in, own_out):
        before.wait()
        after.start()

    own_out[0].wait()
    for k in order:
        pre_sent[k].wait_recv()

    def ring_step(way, step):
        block = (y + RING - step) % RING if way == 0 else (y + step) % RING
        part = pre_out.at[:, rows(block, PRE * ROW)]
        return send(part, part, ring_send.at[way, step], ring_recv.at[way, step], up if way == 0 else down)

    steps = {(0, 0): ring_step(0, 0), (1, 0): ring_step(1, 0)}

    def forward(k):
        origin = (s + ROW - k) % ROW
        kv_sent[k].wait_recv()
        kv_fwd[k] = send(kv_out.at[:, rows(ROW + origin, TOK)], kv_out.at[:, rows(origin, TOK)],
                         fwd_send.at[k], fwd_recv.at[k], up)

    forward(4)
    forward(2)
    for step in range(1, 4):
        for way in range(2):
            if (way, step - 1) in steps and (way == 1 or step < 3):
                steps[way, step - 1].wait_recv()
                steps[way, step] = ring_step(way, step)
        if step == 1:
            forward(6)
            forward(3)
        if step == 2:
            forward(5)
            forward(1)
    forward(7)
    steps[0, 2].wait_recv()
    steps[1, 3].wait_recv()
    for k in order:
        q_sent[k].wait_recv()
    for k in range(ROW):
        kv_fwd[k].wait_recv()
    for copy in (*pre_sent.values(), *kv_sent.values(), *q_sent.values(), *kv_fwd.values(),
                 *steps.values()):
        copy.wait_send()
    own_out[1].wait()
    own_out[2].wait()


def attend_kernel(len_ref, q_ref, kv_ref, pre_ref, o_ref):
    block = pl.program_id(0)
    y = lax.axis_index("req") // ROW
    first = y * (ROW * TOK) + block * TOK
    token = first + lax.broadcasted_iota(jnp.int32, (TOK, 1), 0)
    start = jnp.zeros((TOK, 1), jnp.int32)
    end = jnp.int32(0)
    for r in range(REQS):
        end = end + len_ref[0, r]
        start = jnp.where(token >= end, end, start)
    lowest = jnp.maximum(start, token - (WIN - 1))
    offset = token - start
    lane = lax.broadcasted_iota(jnp.int32, (TOK, LANES), 1)
    q = q_ref[...]
    zero = jnp.zeros_like(q)
    both = jnp.concatenate([jnp.where(lane < HEAD, q, zero), jnp.where(lane >= HEAD, q, zero)], axis=0)
    span = WIN + TOK
    window = pl.ds(pl.multiple_of(block * TOK, TOK), span)
    contract = (((1,), (1,)), ((), ()))
    near = lax.dot_general(both, kv_ref[0, window, :], contract, preferred_element_type=jnp.float32)
    far = lax.dot_general(both, pre_ref[0], contract, preferred_element_type=jnp.float32)
    key = first - WIN + lax.broadcasted_iota(jnp.int32, (TOK, span), 1)
    near_mask = (key >= lowest) & (key <= token)
    far_mask = lax.broadcasted_iota(jnp.int32, (TOK, WIN), 1) > offset
    near = jnp.where(near_mask[None], near.reshape(2, TOK, span), -1e30)
    far = jnp.where(far_mask[None], far.reshape(2, TOK, WIN), -1e30)
    top = jnp.maximum(jnp.max(near, axis=-1, keepdims=True), jnp.max(far, axis=-1, keepdims=True))
    scale = 0.125 * 1.4426950408889634
    near = jnp.exp2((near - top) * scale)
    far = jnp.exp2((far - top) * scale)
    total = jnp.sum(near, axis=-1, keepdims=True) + jnp.sum(far, axis=-1, keepdims=True)
    added = jnp.dot(near.astype(jnp.bfloat16).reshape(2 * TOK, span), kv_ref[1, window, :],
                    preferred_element_type=jnp.float32)
    added += jnp.dot(far.astype(jnp.bfloat16).reshape(2 * TOK, WIN), pre_ref[1],
                     preferred_element_type=jnp.float32)
    added = added.reshape(2, TOK, LANES) / total
    o_ref[...] = jnp.where(lane < HEAD, added[0], added[1]).astype(jnp.bfloat16)


def return_kernel(o_ref, out_ref, own, send_sems, recv_sems, local):
    grp, y, s = place()
    own_in = pltpu.make_async_copy(o_ref.at[rows(s, TOK)], own, local.at[0])
    own_in.start()
    barrier = pltpu.get_barrier_semaphore()
    for k in range(1, ROW):
        pl.semaphore_signal(barrier, 1, device_id=(grp, y * ROW + (s + k) % ROW), device_id_type=MESH)
    pl.semaphore_wait(barrier, ROW - 1)
    copies = []
    for k in (4, 2, 6, 3, 5, 1, 7):
        t = (s + k) % ROW
        copy = pltpu.make_async_remote_copy(
            o_ref.at[rows(t, TOK)], out_ref.at[0, :, cols(s)], send_sems.at[k], recv_sems.at[k],
            device_id=(grp, y * ROW + t), device_id_type=MESH)
        copy.start()
        copies.append(copy)
    own_in.wait()
    own_out = pltpu.make_async_copy(own, out_ref.at[0, :, cols(s)], local.at[1])
    own_out.start()
    for copy in copies:
        copy.wait()
    own_out.wait()


def on_device(queries, suffix_kv, prefix_kv, lengths):
    bf16 = jnp.bfloat16
    anywhere = pl.BlockSpec(memory_space=pl.ANY)
    dma = pltpu.SemaphoreType.DMA
    q, kv, pre = pl.pallas_call(
        gather_kernel,
        out_shape=(
            jax.ShapeDtypeStruct((ROW * TOK, LANES), bf16),
            jax.ShapeDtypeStruct((2, 2 * ROW * TOK, LANES), bf16),
            jax.ShapeDtypeStruct((2, WIN, LANES), bf16),
        ),
        in_specs=[anywhere] * 3,
        out_specs=(anywhere,) * 3,
        scratch_shapes=[
            pltpu.VMEM((TOK, LANES), bf16),
            pltpu.VMEM((2, TOK, LANES), bf16),
            pltpu.VMEM((2, PRE, LANES), bf16),
            dma((3, ROW)), dma((3, ROW)), dma((ROW,)), dma((ROW,)),
            dma((2, 4)), dma((2, 4)), dma((6,)),
        ],
        compiler_params=pltpu.CompilerParams(collective_id=0, has_side_effects=True),
        name="gather",
    )(queries, suffix_kv, prefix_kv)
    mixed = pl.pallas_call(
        attend_kernel,
        grid=(ROW,),
        out_shape=jax.ShapeDtypeStruct((ROW * TOK, LANES), bf16),
        in_specs=[
            pl.BlockSpec(memory_space=pltpu.SMEM),
            pl.BlockSpec((TOK, LANES), lambda i: (i, 0)),
            pl.BlockSpec((2, 2 * ROW * TOK, LANES), lambda i: (0, 0, 0)),
            pl.BlockSpec((2, WIN, LANES), lambda i: (0, 0, 0)),
        ],
        out_specs=pl.BlockSpec((TOK, LANES), lambda i: (i, 0)),
        name="attend",
    )(lengths, q, kv, pre)
    return pl.pallas_call(
        return_kernel,
        out_shape=jax.ShapeDtypeStruct(queries.shape, bf16),
        in_specs=[anywhere],
        out_specs=anywhere,
        scratch_shapes=[pltpu.VMEM((TOK, LANES), bf16), dma((ROW,)), dma((ROW,)), dma((2,))],
        compiler_params=pltpu.CompilerParams(collective_id=1, has_side_effects=True),
        name="give_back",
    )(mixed)


def solution(mesh):
    in_specs = (
        P("grp", "req", None),
        P("grp", None, "req", None),
        P("grp", None, "req", None),
        P("grp", None),
    )
    return jax.shard_map(
        on_device, mesh=mesh, in_specs=in_specs, out_specs=P("grp", "req", None), check_vma=False
    )
```

```python
import functools

import jax
import jax.numpy as jnp
from jax import lax
from jax.experimental import pallas as pl
from jax.experimental.pallas import tpu as pltpu
from jax.sharding import PartitionSpec as P

HEADS = 16
HEAD = 64
WIN = 1024
REQS = 12
ROW = 8
RING = 8
TOK = 128
PRE = 16
LANES = 128
MESH = pl.DeviceIdType.MESH


def place():
    grp = lax.axis_index("grp")
    me = lax.axis_index("req")
    return grp, me // ROW, me % ROW


def cols(number):
    return pl.ds(pl.multiple_of(number * LANES, LANES), LANES)


def rows(number, size, base=0):
    return pl.ds(pl.multiple_of(base + number * size, size), size)


ORDER = (4, 2, 6, 3, 5, 1, 7)
SPAN = WIN + TOK
CONTRACT = (((1,), (1,)), ((), ()))
SCALE = 0.125 * 1.4426950408889634


def whole_kernel(len_ref, q_ref, kv_ref, pre_ref, out_ref,
                 q_all, kv_all, pre_all, acc_all, top_all, sum_all, weight_all, mixed,
                 a2a_send, a2a_recv, fwd_send, fwd_recv, ring_send, ring_recv,
                 back_send, back_recv, local):
    grp, y, s = place()
    up = (grp, ((y + 1) % RING) * ROW + s)
    down = (grp, ((y + RING - 1) % RING) * ROW + s)

    def peer(k):
        return (grp, y * ROW + (s + k) % ROW)

    own = [
        pltpu.make_async_copy(pre_ref.at[0, :, :, cols(s)], pre_all.at[:, rows(y * ROW + s, PRE)], local.at[0]),
        pltpu.make_async_copy(q_ref.at[0, :, cols(s)], q_all.at[rows(s, TOK)], local.at[1]),
        pltpu.make_async_copy(kv_ref.at[0, :, :, cols(s)], kv_all.at[:, rows(ROW + s, TOK)], local.at[2]),
    ]
    for copy in own:
        copy.start()

    barrier = pltpu.get_barrier_semaphore()
    for k in range(1, ROW):
        pl.semaphore_signal(barrier, 1, device_id=peer(k), device_id_type=MESH)
    pl.semaphore_signal(barrier, 1, device_id=up, device_id_type=MESH)
    pl.semaphore_signal(barrier, 1, device_id=down, device_id_type=MESH)
    pl.semaphore_wait(barrier, ROW + 1)

    def send(src, dst, send_sem, recv_sem, to):
        copy = pltpu.make_async_remote_copy(
            src, dst, send_sem, recv_sem, device_id=to, device_id_type=MESH)
        copy.start()
        return copy

    sent = {}
    for k in ORDER:
        t = (s + k) % ROW
        sent[0, k] = send(pre_ref.at[0, :, :, cols(t)], pre_all.at[:, rows(y * ROW + s, PRE)],
                          a2a_send.at[0, k], a2a_recv.at[0, k], peer(k))
    for k in ORDER:
        t = (s + k) % ROW
        sent[1, k] = send(q_ref.at[0, :, cols(t)], q_all.at[rows(s, TOK)],
                          a2a_send.at[1, k], a2a_recv.at[1, k], peer(k))
    for part in range(2):
        for k in ORDER:
            t = (s + k) % ROW
            sent[2 + part, k] = send(
                kv_ref.at[0, part, :, cols(t)], kv_all.at[part, rows(ROW + s, TOK)],
                a2a_send.at[2 + part, k], a2a_recv.at[2 + part, k], peer(k))

    own[0].wait()
    for k in ORDER:
        sent[0, k].wait_recv()
    steps = {}

    def ring_step(way, step):
        block = (y + RING - step) % RING if way == 0 else (y + step) % RING
        part = pre_all.at[:, rows(block, PRE * ROW)]
        steps[way, step] = send(part, part, ring_send.at[way, step], ring_recv.at[way, step],
                                up if way == 0 else down)

    ring_step(0, 0)
    ring_step(1, 0)
    forwarded = {}
    for part in range(2):
        forwarded[part, 0] = send(
            kv_ref.at[0, part, :, cols(s)], kv_all.at[part, rows(s, TOK)],
            fwd_send.at[part, 0], fwd_recv.at[part, 0], up)
    for step in range(1, 4):
        for way in range(2):
            steps[way, step - 1].wait_recv() if (way, step - 1) in steps else None
            if way == 1 or step < 3:
                ring_step(way, step)

    def forward(part, k):
        origin = (s + ROW - k) % ROW
        sent[2 + part, k].wait_recv()
        forwarded[part, k] = send(
            kv_all.at[part, rows(ROW + origin, TOK)], kv_all.at[part, rows(origin, TOK)],
            fwd_send.at[part, k], fwd_recv.at[part, k], up)

    steps[1, 3].wait_recv()
    own[1].wait()
    for k in ORDER:
        sent[1, k].wait_recv()

    def bounds(block):
        first = y * (ROW * TOK) + block * TOK
        token = first + lax.broadcasted_iota(jnp.int32, (TOK, 1), 0)
        start = jnp.zeros((TOK, 1), jnp.int32)
        end = jnp.int32(0)
        for r in range(REQS):
            end = end + len_ref[0, r]
            start = jnp.where(token >= end, end, start)
        return first, token, start

    lane = lax.broadcasted_iota(jnp.int32, (TOK, LANES), 1)

    def two_heads(block):
        q = q_all[rows(block, TOK), :]
        zero = jnp.zeros_like(q)
        return jnp.concatenate(
            [jnp.where(lane < HEAD, q, zero), jnp.where(lane >= HEAD, q, zero)], axis=0)

    def far_block(block, carry):
        first, token, start = bounds(block)
        score = lax.dot_general(two_heads(block), pre_all[0], CONTRACT, preferred_element_type=jnp.float32)
        mask = lax.broadcasted_iota(jnp.int32, (TOK, WIN), 1) > token - start
        score = jnp.where(mask[None], score.reshape(2, TOK, WIN), -1e30).reshape(2 * TOK, WIN)
        top = jnp.max(score, axis=-1, keepdims=True)
        weight = jnp.exp2((score - top) * SCALE)
        here = rows(block, 2 * TOK)
        top_all[here, :] = top
        sum_all[here, :] = jnp.sum(weight, axis=-1, keepdims=True)
        acc_all[here, :] = jnp.dot(weight.astype(jnp.bfloat16), pre_all[1], preferred_element_type=jnp.float32)
        return carry

    def near_block(block, carry):
        first, token, start = bounds(block)
        window = pl.ds(pl.multiple_of(block * TOK, TOK), SPAN)
        score = lax.dot_general(
            two_heads(block), kv_all[0, window, :], CONTRACT, preferred_element_type=jnp.float32)
        key = first - WIN + lax.broadcasted_iota(jnp.int32, (TOK, SPAN), 1)
        mask = (key >= jnp.maximum(start, token - (WIN - 1))) & (key <= token)
        score = jnp.where(mask[None], score.reshape(2, TOK, SPAN), -1e30).reshape(2 * TOK, SPAN)
        here = rows(block, 2 * TOK)
        old = top_all[here, :]
        top = jnp.maximum(old, jnp.max(score, axis=-1, keepdims=True))
        factor = jnp.exp2((old - top) * SCALE)
        weight = jnp.exp2((score - top) * SCALE)
        total = sum_all[here, :] * factor + jnp.sum(weight, axis=-1, keepdims=True)
        weight_all[here, :] = weight.astype(jnp.bfloat16)
        sum_all[here, :] = total
        acc_all[here, :] = acc_all[here, :] * factor
        return carry

    def value_block(block):
        window = pl.ds(pl.multiple_of(block * TOK, TOK), SPAN)
        here = rows(block, 2 * TOK)
        added = acc_all[here, :] + jnp.dot(
            weight_all[here, :], kv_all[1, window, :], preferred_element_type=jnp.float32)
        added = (added / sum_all[here, :]).reshape(2, TOK, LANES)
        mixed[rows(block, TOK), :] = jnp.where(lane < HEAD, added[0], added[1]).astype(jnp.bfloat16)

    for part, blocks in ((0, far_block), (1, near_block)):
        for quarter in range(4):
            lax.fori_loop(2 * quarter, 2 * quarter + 2, blocks, 0)
            for k in ORDER[2 * quarter:2 * quarter + 2]:
                forward(part, k)
        if part == 0:
            own[2].wait()
        for k in range(ROW):
            forwarded[part, k].wait_recv()

    def back(k):
        t = (s + k) % ROW
        return pltpu.make_async_remote_copy(
            mixed.at[rows(t, TOK)], out_ref.at[0, :, cols(s)], back_send.at[k], back_recv.at[k],
            device_id=peer(k), device_id_type=MESH)

    def give_back(k, carry):
        value_block((s + k) % ROW)

        @pl.when(k > 1)
        def _():
            back(k - 1).start()

        return carry

    lax.fori_loop(1, ROW, give_back, 0)
    value_block(s)
    back(ROW - 1).start()
    mine = pltpu.make_async_copy(mixed.at[rows(s, TOK)], out_ref.at[0, :, cols(s)], local.at[3])
    mine.start()
    for copy in (*sent.values(), *forwarded.values(), *steps.values()):
        copy.wait_send()
    for k in range(1, ROW):
        back(k).wait()
    mine.wait()


def on_device(queries, suffix_kv, prefix_kv, lengths):
    bf16 = jnp.bfloat16
    anywhere = pl.BlockSpec(memory_space=pl.ANY)
    dma = pltpu.SemaphoreType.DMA
    tokens = ROW * TOK
    return pl.pallas_call(
        whole_kernel,
        out_shape=jax.ShapeDtypeStruct(queries.shape, bf16),
        in_specs=[pl.BlockSpec(memory_space=pltpu.SMEM)] + [anywhere] * 3,
        out_specs=anywhere,
        scratch_shapes=[
            pltpu.VMEM((tokens, LANES), bf16),
            pltpu.VMEM((2, 2 * tokens, LANES), bf16),
            pltpu.VMEM((2, WIN, LANES), bf16),
            pltpu.VMEM((2 * tokens, LANES), jnp.float32),
            pltpu.VMEM((2 * tokens, 1), jnp.float32),
            pltpu.VMEM((2 * tokens, 1), jnp.float32),
            pltpu.VMEM((2 * tokens, SPAN), bf16),
            pltpu.VMEM((tokens, LANES), bf16),
            dma((4, ROW)), dma((4, ROW)), dma((2, ROW)), dma((2, ROW)),
            dma((2, 4)), dma((2, 4)), dma((ROW,)), dma((ROW,)), dma((4,)),
        ],
        compiler_params=pltpu.CompilerParams(collective_id=0, has_side_effects=True),
        name="suffix_attention",
    )(lengths, queries, suffix_kv, prefix_kv)


def solution(mesh):
    in_specs = (
        P("grp", "req", None),
        P("grp", None, "req", None),
        P("grp", None, "req", None),
        P("grp", None),
    )
    return jax.shard_map(
        on_device, mesh=mesh, in_specs=in_specs, out_specs=P("grp", "req", None), check_vma=False
    )
```

```python
import functools

import jax
import jax.numpy as jnp
from jax import lax
from jax.experimental import pallas as pl
from jax.experimental.pallas import tpu as pltpu
from jax.sharding import PartitionSpec as P

HEADS = 16
HEAD = 64
WIN = 1024
REQS = 12
ROW = 8
RING = 8
TOK = 128
PRE = 16
LANES = 128
MESH = pl.DeviceIdType.MESH


def place():
    grp = lax.axis_index("grp")
    me = lax.axis_index("req")
    return grp, me // ROW, me % ROW


def cols(number):
    return pl.ds(pl.multiple_of(number * LANES, LANES), LANES)


def rows(number, size, base=0):
    return pl.ds(pl.multiple_of(base + number * size, size), size)


ORDER = (4, 2, 6, 3, 5, 1, 7)
SPAN = WIN + TOK
CONTRACT = (((1,), (1,)), ((), ()))
SCALE = 0.125 * 1.4426950408889634


def whole_kernel(len_ref, q_ref, kv_ref, pre_ref, out_ref,
                 q_all, kv_all, pre_all, acc_all, top_all, sum_all, weight_all, mixed,
                 a2a_send, a2a_recv, fwd_send, fwd_recv, ring_send, ring_recv,
                 back_send, back_recv, local):
    grp, y, s = place()
    up = (grp, ((y + 1) % RING) * ROW + s)
    down = (grp, ((y + RING - 1) % RING) * ROW + s)

    def peer(k):
        return (grp, y * ROW + (s + k) % ROW)

    own = [
        pltpu.make_async_copy(pre_ref.at[0, :, :, cols(s)], pre_all.at[:, rows(y * ROW + s, PRE)], local.at[0]),
        pltpu.make_async_copy(q_ref.at[0, :, cols(s)], q_all.at[rows(s, TOK)], local.at[1]),
        pltpu.make_async_copy(kv_ref.at[0, :, :, cols(s)], kv_all.at[:, rows(ROW + s, TOK)], local.at[2]),
    ]
    for copy in own:
        copy.start()

    barrier = pltpu.get_barrier_semaphore()
    for k in range(1, ROW):
        pl.semaphore_signal(barrier, 1, device_id=peer(k), device_id_type=MESH)
    pl.semaphore_signal(barrier, 1, device_id=up, device_id_type=MESH)
    pl.semaphore_signal(barrier, 1, device_id=down, device_id_type=MESH)
    pl.semaphore_wait(barrier, ROW + 1)

    def send(src, dst, send_sem, recv_sem, to):
        copy = pltpu.make_async_remote_copy(
            src, dst, send_sem, recv_sem, device_id=to, device_id_type=MESH)
        copy.start()
        return copy

    sent = {}
    for k in ORDER:
        t = (s + k) % ROW
        sent[0, k] = send(pre_ref.at[0, :, :, cols(t)], pre_all.at[:, rows(y * ROW + s, PRE)],
                          a2a_send.at[0, k], a2a_recv.at[0, k], peer(k))
    for k in ORDER:
        t = (s + k) % ROW
        sent[1, k] = send(q_ref.at[0, :, cols(t)], q_all.at[rows(s, TOK)],
                          a2a_send.at[1, k], a2a_recv.at[1, k], peer(k))
    for part in range(2):
        for k in ORDER:
            t = (s + k) % ROW
            sent[2 + part, k] = send(
                kv_ref.at[0, part, :, cols(t)], kv_all.at[part, rows(ROW + s, TOK)],
                a2a_send.at[2 + part, k], a2a_recv.at[2 + part, k], peer(k))

    own[0].wait()
    for k in ORDER:
        sent[0, k].wait_recv()
    steps = {}

    def ring_step(way, step, half):
        block = (y + RING - step) % RING if way == 0 else (y + step) % RING
        part = pre_all.at[half, rows(block, PRE * ROW)]
        steps[way, step, half] = send(
            part, part, ring_send.at[way, step, half], ring_recv.at[way, step, half],
            up if way == 0 else down)

    def ring_round(step):
        for half in range(2):
            for way in range(2):
                if step and (way == 1 or step < 4):
                    steps[way, step - 1, half].wait_recv()
                if step < 3 + way:
                    ring_step(way, step, half)

    forwarded = {}

    def forward(part, k):
        if k == 0:
            source = kv_ref.at[0, part, :, cols(s)]
        else:
            sent[2 + part, k].wait_recv()
            source = kv_all.at[part, rows(ROW + (s + ROW - k) % ROW, TOK)]
        forwarded[part, k] = send(
            source, kv_all.at[part, rows((s + ROW - k) % ROW, TOK)],
            fwd_send.at[part, k], fwd_recv.at[part, k], up)

    ring_round(0)
    forward(0, 0)
    ring_round(1)
    forward(1, 0)
    ring_round(2)
    for k in ORDER[:3]:
        forward(0, k)
    ring_round(3)
    for k in ORDER[3:]:
        forward(0, k)
    own[1].wait()
    for k in ORDER:
        sent[1, k].wait_recv()
    ring_round(4)

    def bounds(block):
        first = y * (ROW * TOK) + block * TOK
        token = first + lax.broadcasted_iota(jnp.int32, (TOK, 1), 0)
        start = jnp.zeros((TOK, 1), jnp.int32)
        end = jnp.int32(0)
        for r in range(REQS):
            end = end + len_ref[0, r]
            start = jnp.where(token >= end, end, start)
        return first, token, start

    lane = lax.broadcasted_iota(jnp.int32, (TOK, LANES), 1)

    def two_heads(block):
        q = q_all[rows(block, TOK), :]
        zero = jnp.zeros_like(q)
        return jnp.concatenate(
            [jnp.where(lane < HEAD, q, zero), jnp.where(lane >= HEAD, q, zero)], axis=0)

    def far_block(block, carry):
        first, token, start = bounds(block)
        score = lax.dot_general(two_heads(block), pre_all[0], CONTRACT, preferred_element_type=jnp.float32)
        mask = lax.broadcasted_iota(jnp.int32, (TOK, WIN), 1) > token - start
        score = jnp.where(mask[None], score.reshape(2, TOK, WIN), -1e30).reshape(2 * TOK, WIN)
        top = jnp.max(score, axis=-1, keepdims=True)
        weight = jnp.exp2((score - top) * SCALE)
        here = rows(block, 2 * TOK)
        top_all[here, :] = top
        sum_all[here, :] = jnp.sum(weight, axis=-1, keepdims=True)
        acc_all[here, :] = jnp.dot(weight.astype(jnp.bfloat16), pre_all[1], preferred_element_type=jnp.float32)
        return carry

    def near_block(block, carry):
        first, token, start = bounds(block)
        window = pl.ds(pl.multiple_of(block * TOK, TOK), SPAN)
        score = lax.dot_general(
            two_heads(block), kv_all[0, window, :], CONTRACT, preferred_element_type=jnp.float32)
        key = first - WIN + lax.broadcasted_iota(jnp.int32, (TOK, SPAN), 1)
        mask = (key >= jnp.maximum(start, token - (WIN - 1))) & (key <= token)
        score = jnp.where(mask[None], score.reshape(2, TOK, SPAN), -1e30).reshape(2 * TOK, SPAN)
        here = rows(block, 2 * TOK)
        old = top_all[here, :]
        top = jnp.maximum(old, jnp.max(score, axis=-1, keepdims=True))
        factor = jnp.exp2((old - top) * SCALE)
        weight = jnp.exp2((score - top) * SCALE)
        total = sum_all[here, :] * factor + jnp.sum(weight, axis=-1, keepdims=True)
        weight_all[here, :] = weight.astype(jnp.bfloat16)
        sum_all[here, :] = total
        acc_all[here, :] = acc_all[here, :] * factor
        return carry

    def value_block(block):
        window = pl.ds(pl.multiple_of(block * TOK, TOK), SPAN)
        here = rows(block, 2 * TOK)
        added = acc_all[here, :] + jnp.dot(
            weight_all[here, :], kv_all[1, window, :], preferred_element_type=jnp.float32)
        added = (added / sum_all[here, :]).reshape(2, TOK, LANES)
        mixed[rows(block, TOK), :] = jnp.where(lane < HEAD, added[0], added[1]).astype(jnp.bfloat16)

    for quarter in range(4):
        lax.fori_loop(2 * quarter, 2 * quarter + 2, far_block, 0)
        for k in ORDER[2 * quarter:2 * quarter + 2]:
            forward(1, k)
    own[2].wait()
    for k in range(ROW):
        forwarded[0, k].wait_recv()

    def back(k):
        t = (s + k) % ROW
        return pltpu.make_async_remote_copy(
            mixed.at[rows(t, TOK)], out_ref.at[0, :, cols(s)], back_send.at[k], back_recv.at[k],
            device_id=peer(k), device_id_type=MESH)

    def near_first(k, carry):
        return near_block((s + k) % ROW, carry)

    def near_and_back(k, carry):
        value_block((s + k) % ROW)
        near_block((s + k + 4) % ROW, carry)
        back(k).start()
        return carry

    def late_back(k, carry):
        value_block((s + k) % ROW)

        @pl.when(k > 5)
        def _():
            back(k - 1).start()

        return carry

    lax.fori_loop(1, 5, near_first, 0)
    for k in range(ROW):
        forwarded[1, k].wait_recv()
    lax.fori_loop(1, 5, near_and_back, 0)
    lax.fori_loop(5, ROW, late_back, 0)
    value_block(s)
    back(ROW - 1).start()
    mine = pltpu.make_async_copy(mixed.at[rows(s, TOK)], out_ref.at[0, :, cols(s)], local.at[3])
    mine.start()
    for copy in (*sent.values(), *forwarded.values(), *steps.values()):
        copy.wait_send()
    for k in range(1, ROW):
        back(k).wait()
    mine.wait()


def on_device(queries, suffix_kv, prefix_kv, lengths):
    bf16 = jnp.bfloat16
    anywhere = pl.BlockSpec(memory_space=pl.ANY)
    dma = pltpu.SemaphoreType.DMA
    tokens = ROW * TOK
    return pl.pallas_call(
        whole_kernel,
        out_shape=jax.ShapeDtypeStruct(queries.shape, bf16),
        in_specs=[pl.BlockSpec(memory_space=pltpu.SMEM)] + [anywhere] * 3,
        out_specs=anywhere,
        scratch_shapes=[
            pltpu.VMEM((tokens, LANES), bf16),
            pltpu.VMEM((2, 2 * tokens, LANES), bf16),
            pltpu.VMEM((2, WIN, LANES), bf16),
            pltpu.VMEM((2 * tokens, LANES), jnp.float32),
            pltpu.VMEM((2 * tokens, 1), jnp.float32),
            pltpu.VMEM((2 * tokens, 1), jnp.float32),
            pltpu.VMEM((2 * tokens, SPAN), bf16),
            pltpu.VMEM((tokens, LANES), bf16),
            dma((4, ROW)), dma((4, ROW)), dma((2, ROW)), dma((2, ROW)),
            dma((2, 4, 2)), dma((2, 4, 2)), dma((ROW,)), dma((ROW,)), dma((4,)),
        ],
        compiler_params=pltpu.CompilerParams(collective_id=0, has_side_effects=True),
        name="suffix_attention",
    )(lengths, queries, suffix_kv, prefix_kv)


def solution(mesh):
    in_specs = (
        P("grp", "req", None),
        P("grp", None, "req", None),
        P("grp", None, "req", None),
        P("grp", None),
    )
    return jax.shard_map(
        on_device, mesh=mesh, in_specs=in_specs, out_specs=P("grp", "req", None), check_vma=False
    )
```

```python
import functools

import jax
import jax.numpy as jnp
from jax import lax
from jax.experimental import pallas as pl
from jax.experimental.pallas import tpu as pltpu
from jax.sharding import PartitionSpec as P

HEADS = 16
HEAD = 64
WIN = 1024
REQS = 12
ROW = 8
RING = 8
TOK = 128
PRE = 16
LANES = 128
MESH = pl.DeviceIdType.MESH


def place():
    grp = lax.axis_index("grp")
    me = lax.axis_index("req")
    return grp, me // ROW, me % ROW


def cols(number):
    return pl.ds(pl.multiple_of(number * LANES, LANES), LANES)


def rows(number, size, base=0):
    return pl.ds(pl.multiple_of(base + number * size, size), size)


ORDER = (4, 2, 6, 3, 5, 1, 7)
SPAN = WIN + TOK
CONTRACT = (((1,), (1,)), ((), ()))
SCALE = 0.125 * 1.4426950408889634


def whole_kernel(len_ref, q_ref, kv_ref, pre_ref, out_ref,
                 q_all, kv_all, pre_all, acc_all, top_all, sum_all, weight_all, mixed,
                 a2a_send, a2a_recv, fwd_send, fwd_recv, ring_send, ring_recv,
                 back_send, back_recv, local):
    grp, y, s = place()
    up = (grp, ((y + 1) % RING) * ROW + s)
    down = (grp, ((y + RING - 1) % RING) * ROW + s)

    def peer(k):
        return (grp, y * ROW + (s + k) % ROW)

    own = [
        pltpu.make_async_copy(pre_ref.at[0, :, :, cols(s)], pre_all.at[:, rows(y * ROW + s, PRE)], local.at[0]),
        pltpu.make_async_copy(q_ref.at[0, :, cols(s)], q_all.at[rows(s, TOK)], local.at[1]),
        pltpu.make_async_copy(kv_ref.at[0, :, :, cols(s)], kv_all.at[:, rows(ROW + s, TOK)], local.at[2]),
    ]
    for copy in own:
        copy.start()

    barrier = pltpu.get_barrier_semaphore()
    for k in range(1, ROW):
        pl.semaphore_signal(barrier, 1, device_id=peer(k), device_id_type=MESH)
    pl.semaphore_signal(barrier, 1, device_id=up, device_id_type=MESH)
    pl.semaphore_signal(barrier, 1, device_id=down, device_id_type=MESH)
    pl.semaphore_wait(barrier, ROW + 1)

    def send(src, dst, send_sem, recv_sem, to):
        copy = pltpu.make_async_remote_copy(
            src, dst, send_sem, recv_sem, device_id=to, device_id_type=MESH)
        copy.start()
        return copy

    sent = {}
    for k in ORDER:
        t = (s + k) % ROW
        sent[0, k] = send(pre_ref.at[0, :, :, cols(t)], pre_all.at[:, rows(y * ROW + s, PRE)],
                          a2a_send.at[0, k], a2a_recv.at[0, k], peer(k))
    for k in ORDER:
        t = (s + k) % ROW
        sent[1, k] = send(q_ref.at[0, :, cols(t)], q_all.at[rows(s, TOK)],
                          a2a_send.at[1, k], a2a_recv.at[1, k], peer(k))
    own[0].wait()
    for k in ORDER:
        sent[0, k].wait_recv()
    steps = {}

    def ring_step(way, step, half):
        block = (y + RING - step) % RING if way == 0 else (y + step) % RING
        part = pre_all.at[half, rows(block, PRE * ROW)]
        steps[way, step, half] = send(
            part, part, ring_send.at[way, step, half], ring_recv.at[way, step, half],
            up if way == 0 else down)

    def ring_round(step):
        for half in range(2):
            for way in range(2):
                if step and (way == 1 or step < 4):
                    steps[way, step - 1, half].wait_recv()
                if step < 3 + way:
                    ring_step(way, step, half)

    forwarded = {}

    def forward(part, k):
        if k == 0:
            source = kv_ref.at[0, part, :, cols(s)]
        else:
            sent[2 + part, k].wait_recv()
            source = kv_all.at[part, rows(ROW + (s + ROW - k) % ROW, TOK)]
        forwarded[part, k] = send(
            source, kv_all.at[part, rows((s + ROW - k) % ROW, TOK)],
            fwd_send.at[part, k], fwd_recv.at[part, k], up)

    for part in range(1):
        for k in ORDER:
            t = (s + k) % ROW
            sent[2 + part, k] = send(
                kv_ref.at[0, part, :, cols(t)], kv_all.at[part, rows(ROW + s, TOK)],
                a2a_send.at[2 + part, k], a2a_recv.at[2 + part, k], peer(k))

    ring_round(0)
    forward(0, 0)
    ring_round(1)
    forward(1, 0)
    ring_round(2)
    for k in ORDER[:3]:
        forward(0, k)
    for part in range(1, 2):
        for k in ORDER:
            t = (s + k) % ROW
            sent[2 + part, k] = send(
                kv_ref.at[0, part, :, cols(t)], kv_all.at[part, rows(ROW + s, TOK)],
                a2a_send.at[2 + part, k], a2a_recv.at[2 + part, k], peer(k))

    ring_round(3)
    for k in ORDER[3:]:
        forward(0, k)
    own[1].wait()
    for k in ORDER:
        sent[1, k].wait_recv()
    ring_round(4)

    def bounds(block):
        first = y * (ROW * TOK) + block * TOK
        token = first + lax.broadcasted_iota(jnp.int32, (TOK, 1), 0)
        start = jnp.zeros((TOK, 1), jnp.int32)
        end = jnp.int32(0)
        for r in range(REQS):
            end = end + len_ref[0, r]
            start = jnp.where(token >= end, end, start)
        return first, token, start

    lane = lax.broadcasted_iota(jnp.int32, (TOK, LANES), 1)

    def two_heads(block):
        q = q_all[rows(block, TOK), :]
        zero = jnp.zeros_like(q)
        return jnp.concatenate(
            [jnp.where(lane < HEAD, q, zero), jnp.where(lane >= HEAD, q, zero)], axis=0)

    def far_block(block, carry):
        first, token, start = bounds(block)
        score = lax.dot_general(two_heads(block), pre_all[0], CONTRACT, preferred_element_type=jnp.float32)
        mask = lax.broadcasted_iota(jnp.int32, (TOK, WIN), 1) > token - start
        score = jnp.where(mask[None], score.reshape(2, TOK, WIN), -1e30).reshape(2 * TOK, WIN)
        top = jnp.max(score, axis=-1, keepdims=True)
        weight = jnp.exp2((score - top) * SCALE)
        here = rows(block, 2 * TOK)
        top_all[here, :] = top
        sum_all[here, :] = jnp.sum(weight, axis=-1, keepdims=True)
        acc_all[here, :] = jnp.dot(weight.astype(jnp.bfloat16), pre_all[1], preferred_element_type=jnp.float32)
        return carry

    def near_block(block, carry):
        first, token, start = bounds(block)
        window = pl.ds(pl.multiple_of(block * TOK, TOK), SPAN)
        score = lax.dot_general(
            two_heads(block), kv_all[0, window, :], CONTRACT, preferred_element_type=jnp.float32)
        key = first - WIN + lax.broadcasted_iota(jnp.int32, (TOK, SPAN), 1)
        mask = (key >= jnp.maximum(start, token - (WIN - 1))) & (key <= token)
        score = jnp.where(mask[None], score.reshape(2, TOK, SPAN), -1e30).reshape(2 * TOK, SPAN)
        here = rows(block, 2 * TOK)
        old = top_all[here, :]
        top = jnp.maximum(old, jnp.max(score, axis=-1, keepdims=True))
        factor = jnp.exp2((old - top) * SCALE)
        weight = jnp.exp2((score - top) * SCALE)
        total = sum_all[here, :] * factor + jnp.sum(weight, axis=-1, keepdims=True)
        weight_all[here, :] = weight.astype(jnp.bfloat16)
        sum_all[here, :] = total
        acc_all[here, :] = acc_all[here, :] * factor
        return carry

    def value_block(block):
        window = pl.ds(pl.multiple_of(block * TOK, TOK), SPAN)
        here = rows(block, 2 * TOK)
        added = acc_all[here, :] + jnp.dot(
            weight_all[here, :], kv_all[1, window, :], preferred_element_type=jnp.float32)
        added = (added / sum_all[here, :]).reshape(2, TOK, LANES)
        mixed[rows(block, TOK), :] = jnp.where(lane < HEAD, added[0], added[1]).astype(jnp.bfloat16)

    for quarter in range(4):
        lax.fori_loop(2 * quarter, 2 * quarter + 2, far_block, 0)
        for k in ORDER[2 * quarter:2 * quarter + 2]:
            forward(1, k)
    own[2].wait()
    for k in range(ROW):
        forwarded[0, k].wait_recv()

    def back(k):
        t = (s + k) % ROW
        return pltpu.make_async_remote_copy(
            mixed.at[rows(t, TOK)], out_ref.at[0, :, cols(s)], back_send.at[k], back_recv.at[k],
            device_id=peer(k), device_id_type=MESH)

    def near_first(k, carry):
        return near_block((s + k) % ROW, carry)

    def near_and_back(k, carry):
        value_block((s + k) % ROW)
        near_block((s + k + 4) % ROW, carry)
        back(k).start()
        return carry

    def late_back(k, carry):
        value_block((s + k) % ROW)

        @pl.when(k > 5)
        def _():
            back(k - 1).start()

        return carry

    lax.fori_loop(1, 5, near_first, 0)
    for k in range(ROW):
        forwarded[1, k].wait_recv()
    lax.fori_loop(1, 5, near_and_back, 0)
    lax.fori_loop(5, ROW, late_back, 0)
    value_block(s)
    back(ROW - 1).start()
    mine = pltpu.make_async_copy(mixed.at[rows(s, TOK)], out_ref.at[0, :, cols(s)], local.at[3])
    mine.start()
    for copy in (*sent.values(), *forwarded.values(), *steps.values()):
        copy.wait_send()
    for k in range(1, ROW):
        back(k).wait()
    mine.wait()


def on_device(queries, suffix_kv, prefix_kv, lengths):
    bf16 = jnp.bfloat16
    anywhere = pl.BlockSpec(memory_space=pl.ANY)
    dma = pltpu.SemaphoreType.DMA
    tokens = ROW * TOK
    return pl.pallas_call(
        whole_kernel,
        out_shape=jax.ShapeDtypeStruct(queries.shape, bf16),
        in_specs=[pl.BlockSpec(memory_space=pltpu.SMEM)] + [anywhere] * 3,
        out_specs=anywhere,
        scratch_shapes=[
            pltpu.VMEM((tokens, LANES), bf16),
            pltpu.VMEM((2, 2 * tokens, LANES), bf16),
            pltpu.VMEM((2, WIN, LANES), bf16),
            pltpu.VMEM((2 * tokens, LANES), jnp.float32),
            pltpu.VMEM((2 * tokens, 1), jnp.float32),
            pltpu.VMEM((2 * tokens, 1), jnp.float32),
            pltpu.VMEM((2 * tokens, SPAN), bf16),
            pltpu.VMEM((tokens, LANES), bf16),
            dma((4, ROW)), dma((4, ROW)), dma((2, ROW)), dma((2, ROW)),
            dma((2, 4, 2)), dma((2, 4, 2)), dma((ROW,)), dma((ROW,)), dma((4,)),
        ],
        compiler_params=pltpu.CompilerParams(collective_id=0, has_side_effects=True),
        name="suffix_attention",
    )(lengths, queries, suffix_kv, prefix_kv)


def solution(mesh):
    in_specs = (
        P("grp", "req", None),
        P("grp", None, "req", None),
        P("grp", None, "req", None),
        P("grp", None),
    )
    return jax.shard_map(
        on_device, mesh=mesh, in_specs=in_specs, out_specs=P("grp", "req", None), check_vma=False
    )
```

```python
import functools

import jax
import jax.numpy as jnp
from jax import lax
from jax.experimental import pallas as pl
from jax.experimental.pallas import tpu as pltpu
from jax.sharding import PartitionSpec as P

HEADS = 16
HEAD = 64
WIN = 1024
REQS = 12
ROW = 8
RING = 8
TOK = 128
PRE = 16
LANES = 128
MESH = pl.DeviceIdType.MESH


def place():
    grp = lax.axis_index("grp")
    me = lax.axis_index("req")
    return grp, me // ROW, me % ROW


def cols(number):
    return pl.ds(pl.multiple_of(number * LANES, LANES), LANES)


def rows(number, size, base=0):
    return pl.ds(pl.multiple_of(base + number * size, size), size)


ORDER = (2, 6, 4, 1, 7, 3, 5)
SPAN = WIN + TOK
CONTRACT = (((1,), (1,)), ((), ()))
SCALE = 0.125 * 1.4426950408889634


def whole_kernel(len_ref, q_ref, kv_ref, pre_ref, out_ref,
                 q_all, kv_all, pre_all, acc_all, top_all, sum_all, weight_all, mixed,
                 a2a_send, a2a_recv, fwd_send, fwd_recv, ring_send, ring_recv,
                 back_send, back_recv, local):
    grp, y, s = place()
    up = (grp, ((y + 1) % RING) * ROW + s)
    down = (grp, ((y + RING - 1) % RING) * ROW + s)

    def peer(k):
        return (grp, y * ROW + (s + k) % ROW)

    own = [
        pltpu.make_async_copy(pre_ref.at[0, :, :, cols(s)], pre_all.at[:, rows(y * ROW + s, PRE)], local.at[0]),
        pltpu.make_async_copy(q_ref.at[0, :, cols(s)], q_all.at[rows(s, TOK)], local.at[1]),
        pltpu.make_async_copy(kv_ref.at[0, :, :, cols(s)], kv_all.at[:, rows(ROW + s, TOK)], local.at[2]),
    ]
    for copy in own:
        copy.start()

    barrier = pltpu.get_barrier_semaphore()
    for k in range(1, ROW):
        pl.semaphore_signal(barrier, 1, device_id=peer(k), device_id_type=MESH)
    pl.semaphore_signal(barrier, 1, device_id=up, device_id_type=MESH)
    pl.semaphore_signal(barrier, 1, device_id=down, device_id_type=MESH)
    pl.semaphore_wait(barrier, ROW + 1)

    def send(src, dst, send_sem, recv_sem, to):
        copy = pltpu.make_async_remote_copy(
            src, dst, send_sem, recv_sem, device_id=to, device_id_type=MESH)
        copy.start()
        return copy

    sent = {}
    for k in ORDER:
        t = (s + k) % ROW
        sent[0, k] = send(pre_ref.at[0, :, :, cols(t)], pre_all.at[:, rows(y * ROW + s, PRE)],
                          a2a_send.at[0, k], a2a_recv.at[0, k], peer(k))
    for k in ORDER:
        t = (s + k) % ROW
        sent[1, k] = send(q_ref.at[0, :, cols(t)], q_all.at[rows(s, TOK)],
                          a2a_send.at[1, k], a2a_recv.at[1, k], peer(k))
    own[0].wait()
    for k in ORDER:
        sent[0, k].wait_recv()
    steps = {}

    def ring_step(way, step, half):
        block = (y + RING - step) % RING if way == 0 else (y + step) % RING
        part = pre_all.at[half, rows(block, PRE * ROW)]
        steps[way, step, half] = send(
            part, part, ring_send.at[way, step, half], ring_recv.at[way, step, half],
            up if way == 0 else down)

    def ring_round(step):
        for half in range(2):
            for way in range(2):
                if step and (way == 1 or step < 4):
                    steps[way, step - 1, half].wait_recv()
                if step < 3 + way:
                    ring_step(way, step, half)

    forwarded = {}

    def forward(part, k):
        if k == 0:
            source = kv_ref.at[0, part, :, cols(s)]
        else:
            sent[2 + part, k].wait_recv()
            source = kv_all.at[part, rows(ROW + (s + ROW - k) % ROW, TOK)]
        forwarded[part, k] = send(
            source, kv_all.at[part, rows((s + ROW - k) % ROW, TOK)],
            fwd_send.at[part, k], fwd_recv.at[part, k], up)

    for part in range(1):
        for k in ORDER:
            t = (s + k) % ROW
            sent[2 + part, k] = send(
                kv_ref.at[0, part, :, cols(t)], kv_all.at[part, rows(ROW + s, TOK)],
                a2a_send.at[2 + part, k], a2a_recv.at[2 + part, k], peer(k))

    ring_round(0)
    forward(0, 0)
    ring_round(1)
    forward(1, 0)
    ring_round(2)
    for k in ORDER[:3]:
        forward(0, k)
    for part in range(1, 2):
        for k in ORDER:
            t = (s + k) % ROW
            sent[2 + part, k] = send(
                kv_ref.at[0, part, :, cols(t)], kv_all.at[part, rows(ROW + s, TOK)],
                a2a_send.at[2 + part, k], a2a_recv.at[2 + part, k], peer(k))

    ring_round(3)
    for k in ORDER[3:]:
        forward(0, k)
    own[1].wait()
    for k in ORDER:
        sent[1, k].wait_recv()
    ring_round(4)

    def bounds(block):
        first = y * (ROW * TOK) + block * TOK
        token = first + lax.broadcasted_iota(jnp.int32, (TOK, 1), 0)
        start = jnp.zeros((TOK, 1), jnp.int32)
        end = jnp.int32(0)
        for r in range(REQS):
            end = end + len_ref[0, r]
            start = jnp.where(token >= end, end, start)
        return first, token, start

    lane = lax.broadcasted_iota(jnp.int32, (TOK, LANES), 1)

    def two_heads(block):
        q = q_all[rows(block, TOK), :]
        zero = jnp.zeros_like(q)
        return jnp.concatenate(
            [jnp.where(lane < HEAD, q, zero), jnp.where(lane >= HEAD, q, zero)], axis=0)

    def far_block(block, carry):
        first, token, start = bounds(block)
        score = lax.dot_general(two_heads(block), pre_all[0], CONTRACT, preferred_element_type=jnp.float32)
        mask = lax.broadcasted_iota(jnp.int32, (TOK, WIN), 1) > token - start
        score = jnp.where(mask[None], score.reshape(2, TOK, WIN), -1e30).reshape(2 * TOK, WIN)
        top = jnp.max(score, axis=-1, keepdims=True)
        weight = jnp.exp2((score - top) * SCALE)
        here = rows(block, 2 * TOK)
        top_all[here, :] = top
        sum_all[here, :] = jnp.sum(weight, axis=-1, keepdims=True)
        acc_all[here, :] = jnp.dot(weight.astype(jnp.bfloat16), pre_all[1], preferred_element_type=jnp.float32)
        return carry

    def near_block(block, carry):
        first, token, start = bounds(block)
        window = pl.ds(pl.multiple_of(block * TOK, TOK), SPAN)
        score = lax.dot_general(
            two_heads(block), kv_all[0, window, :], CONTRACT, preferred_element_type=jnp.float32)
        key = first - WIN + lax.broadcasted_iota(jnp.int32, (TOK, SPAN), 1)
        mask = (key >= jnp.maximum(start, token - (WIN - 1))) & (key <= token)
        score = jnp.where(mask[None], score.reshape(2, TOK, SPAN), -1e30).reshape(2 * TOK, SPAN)
        here = rows(block, 2 * TOK)
        old = top_all[here, :]
        top = jnp.maximum(old, jnp.max(score, axis=-1, keepdims=True))
        factor = jnp.exp2((old - top) * SCALE)
        weight = jnp.exp2((score - top) * SCALE)
        total = sum_all[here, :] * factor + jnp.sum(weight, axis=-1, keepdims=True)
        weight_all[here, :] = weight.astype(jnp.bfloat16)
        sum_all[here, :] = total
        acc_all[here, :] = acc_all[here, :] * factor
        return carry

    def value_block(block):
        window = pl.ds(pl.multiple_of(block * TOK, TOK), SPAN)
        here = rows(block, 2 * TOK)
        added = acc_all[here, :] + jnp.dot(
            weight_all[here, :], kv_all[1, window, :], preferred_element_type=jnp.float32)
        added = (added / sum_all[here, :]).reshape(2, TOK, LANES)
        mixed[rows(block, TOK), :] = jnp.where(lane < HEAD, added[0], added[1]).astype(jnp.bfloat16)

    for quarter in range(4):
        lax.fori_loop(2 * quarter, 2 * quarter + 2, far_block, 0)
        for k in ORDER[2 * quarter:2 * quarter + 2]:
            forward(1, k)
    own[2].wait()
    for k in range(ROW):
        forwarded[0, k].wait_recv()

    def back(k):
        t = (s + k) % ROW
        return pltpu.make_async_remote_copy(
            mixed.at[rows(t, TOK)], out_ref.at[0, :, cols(s)], back_send.at[k], back_recv.at[k],
            device_id=peer(k), device_id_type=MESH)

    def near_first(k, carry):
        return near_block((s + k) % ROW, carry)

    def near_and_back(k, carry):
        value_block((s + k) % ROW)
        near_block((s + k + 2) % ROW, carry)
        back(k).start()
        return carry

    lax.fori_loop(1, 3, near_first, 0)
    for k in range(ROW):
        forwarded[1, k].wait_recv()
    lax.fori_loop(1, 7, near_and_back, 0)
    value_block((s + ROW - 1) % ROW)
    value_block(s)
    back(ROW - 1).start()
    mine = pltpu.make_async_copy(mixed.at[rows(s, TOK)], out_ref.at[0, :, cols(s)], local.at[3])
    mine.start()
    for copy in (*sent.values(), *forwarded.values(), *steps.values()):
        copy.wait_send()
    for k in range(1, ROW):
        back(k).wait()
    mine.wait()


def on_device(queries, suffix_kv, prefix_kv, lengths):
    bf16 = jnp.bfloat16
    anywhere = pl.BlockSpec(memory_space=pl.ANY)
    dma = pltpu.SemaphoreType.DMA
    tokens = ROW * TOK
    return pl.pallas_call(
        whole_kernel,
        out_shape=jax.ShapeDtypeStruct(queries.shape, bf16),
        in_specs=[pl.BlockSpec(memory_space=pltpu.SMEM)] + [anywhere] * 3,
        out_specs=anywhere,
        scratch_shapes=[
            pltpu.VMEM((tokens, LANES), bf16),
            pltpu.VMEM((2, 2 * tokens, LANES), bf16),
            pltpu.VMEM((2, WIN, LANES), bf16),
            pltpu.VMEM((2 * tokens, LANES), jnp.float32),
            pltpu.VMEM((2 * tokens, 1), jnp.float32),
            pltpu.VMEM((2 * tokens, 1), jnp.float32),
            pltpu.VMEM((2 * tokens, SPAN), bf16),
            pltpu.VMEM((tokens, LANES), bf16),
            dma((4, ROW)), dma((4, ROW)), dma((2, ROW)), dma((2, ROW)),
            dma((2, 4, 2)), dma((2, 4, 2)), dma((ROW,)), dma((ROW,)), dma((4,)),
        ],
        compiler_params=pltpu.CompilerParams(collective_id=0, has_side_effects=True),
        name="suffix_attention",
    )(lengths, queries, suffix_kv, prefix_kv)


def solution(mesh):
    in_specs = (
        P("grp", "req", None),
        P("grp", None, "req", None),
        P("grp", None, "req", None),
        P("grp", None),
    )
    return jax.shard_map(
        on_device, mesh=mesh, in_specs=in_specs, out_specs=P("grp", "req", None), check_vma=False
    )
```
